32 devices in a mesh: seq: 8 (over y, x, core), mlp: 4 (over z).
Axes of the slice: x: 2, y: 2, z: 4, core: 2. Of those that a mesh axis runs over, the one named last changes fastest.
Arguments:
- hidden_in: bfloat16 [36864, 768], P(('seq', 'mlp')), may hold values from -6 to 6
- cotangent: bfloat16 [36864, 768], P(('seq', 'mlp')), may hold values from -6 to 6
- w_qkv: bfloat16 [768, 2304], P(None, ('seq', 'mlp')), may hold values from -0.21875 to 0.21875
- w_attn_out: bfloat16 [768, 768], P(None, ('seq', 'mlp')), may hold values from -2.5 to 2.5
- attn_gain: bfloat16 [768], P(('seq', 'mlp')), may hold values from 0.099609375 to 1.8984375
- mlp_gain: bfloat16 [768], P(('seq', 'mlp')), may hold values from 0.099609375 to 1.8984375
- w_gate: bfloat16 [768, 1152], P(None, 'mlp'), may hold values from -0.21875 to 0.21875
- w_up: bfloat16 [768, 1152], P(None, 'mlp'), may hold values from -0.21875 to 0.21875
- w_down: bfloat16 [1152, 768], P('mlp'), may hold values from -0.1875 to 0.1875
- doc_lengths: int32 [32, 5], P(('seq', 'mlp')), may hold values from 1 to 1024, 1152 in all within a row
Outputs:
- layer_out: bfloat16 [36864, 768], P(('seq', 'mlp'))
- grad_hidden: bfloat16 [36864, 768], P(('seq', 'mlp'))
- grad_qkv: float32 [768, 2304], P(None, ('seq', 'mlp'))
- grad_attn_out: float32 [768, 768], P(None, ('seq', 'mlp'))
- grad_attn_gain: float32 [768], P(('seq', 'mlp'))
- grad_mlp_gain: float32 [768], P(('seq', 'mlp'))
- grad_gate: float32 [768, 1152], P(None, 'mlp')
- grad_up: float32 [768, 1152], P(None, 'mlp')
- grad_down: float32 [1152, 768], P('mlp')
The draws below stay inside these ranges and needn't reach their ends.
Inputs may be any that keep to these rules, and one draw needn't show every extreme that they name: `doc_lengths`: row b gives the lengths of the 4 documents packed in order from the start of block b, then the number of padding rows at its end; a row sums to 1152.
All inputs are finite; a program needn't handle non-finite values.
Results may differ from the reference program's by a relative error of at most 0.015.
Values may be sent and summed in bfloat16 or wider, within the bound.
No kernel may reach another device: no remote copies, remote signals or barrier semaphores. Data moves between devices by JAX's collectives and lax.ppermute only.
A program may use at most 192 MiB of HBM per device.

```python
import math
import jax
import jax.numpy as jnp
import numpy as np
from jax import lax

D = 768
HEADS = 12
HEAD_DIM = 64
FF = 1152
TOK_DEV = 1152
DOCS = 4
SLOTS = 5
LONGEST = 1024
BLOCKS = 32
TOKENS = 36864


def spiked(result, own_key, source, target, parts, factor):
    def block_of(dim):
        return (jnp.arange(result.shape[dim]) // (result.shape[dim] // parts)).reshape((-1,) + (1,) * (result.ndim - 1 - dim))

    near = jax.random.permutation(own_key, parts)[block_of(target)]
    second = (block_of(target) + parts // 2) % parts
    return jnp.where((block_of(source) == near) | (block_of(source) == second), factor * result, result)


def steps_of(rng, extent, shards, smallest, high):
    def one(dim, parts):
        draws = jax.random.uniform(jax.random.fold_in(jax.random.fold_in(rng, 6), dim), (parts,), jnp.float32, smallest / len(shards), high / len(shards))
        return jnp.repeat(jnp.exp(draws), extent[dim] // parts).reshape((-1,) + (1,) * (len(extent) - dim - 1))

    level = one(*shards[0])
    for cut in shards[1:]:
        level = level * one(*cut)
    return level


def profile(count, total, reach, lean):
    portions = [(1 << 20) // math.isqrt(grade ** lean) + 1 for grade in range(2, count + 1)]
    rest, holding = total - reach - (count - 1), [1] * (count - 1)
    while rest > 0:
        free = [i for i in range(count - 1) if holding[i] < reach]
        whole, remaining = sum([portions[i] for i in free]), rest
        for i in free:
            extra = min(reach - holding[i], max(1, remaining * portions[i] // whole), rest)
            holding[i] = holding[i] + extra
            rest = rest - extra
    return np.array([reach] + holding)


def ragged(stream_key, amount, total, reach, lean):
    if amount == 2:
        one = jax.random.randint(stream_key, (), max(1, total - reach), min(reach, total - 1) + 1)
        return jnp.stack([one, total - one])
    lengths = jnp.asarray(profile(amount, total, reach, lean), jnp.int32)
    couples = (amount - 1) // 2
    donor, receiver = lengths[1:1 + 2 * couples:2], lengths[2:2 + 2 * couples:2]
    margin = jnp.minimum(donor - 1, reach - receiver)
    moved = jax.random.randint(jax.random.fold_in(stream_key, 1), (couples,), 0, 1 << 20) % (margin + 1)
    lengths = lengths.at[1:1 + 2 * couples:2].set(donor - moved).at[2:2 + 2 * couples:2].set(receiver + moved)
    return lengths[jax.random.permutation(jax.random.fold_in(stream_key, 2), amount)]


def normal_values(stream_key, extent, deviation, most, pieces=(), kind=jnp.bfloat16):
    loudness = steps_of(stream_key, extent, pieces, -0.22, 0.18) if pieces else 1.0
    result = jax.random.normal(stream_key, extent, jnp.float32) * deviation * loudness
    return jnp.minimum(jnp.maximum(result, -most), most).astype(kind)


def noise_with(stream_key, dims, width, limit, split, heavy, kind=jnp.bfloat16):
    drawn = width * jax.random.normal(stream_key, dims, jnp.float32)
    if split:
        drawn = drawn * steps_of(stream_key, dims, split, -0.22, 0.18)
    return jnp.clip(spiked(drawn, jax.random.fold_in(stream_key, 3), *heavy), -limit, limit).astype(kind)


def setup_inputs(seed: int = 0) -> dict:
    key_list = jax.random.split(jax.random.key(seed), 11)
    return {
        "hidden_in": normal_values(key_list[0], (TOKENS, D), 1.0, 6.0, ((0, 32),)),
        "cotangent": noise_with(key_list[1], (TOKENS, D), 1.0, 6.0, ((0, 32),), (0, 1, 32, 2.75)),
        "w_qkv": normal_values(key_list[2], (D, 3 * D), D ** -0.5, 0.21875, ((1, 32),)),
        "w_attn_out": normal_values(key_list[3], (D, D), (max(1, 8 * D // TOK_DEV)) ** -0.5, 2.5, ((1, 32),)),
        "attn_gain": jnp.clip(1.0 + 0.18 * jax.random.normal(key_list[4], (D,), jnp.float32), 0.099609375, 1.8984375).astype(jnp.bfloat16),
        "mlp_gain": jnp.clip(1.0 + 0.18 * jax.random.normal(key_list[5], (D,), jnp.float32), 0.099609375, 1.8984375).astype(jnp.bfloat16),
        "w_gate": normal_values(key_list[6], (D, FF), D ** -0.5, 0.21875, ((1, 4),)),
        "w_up": normal_values(key_list[7], (D, FF), D ** -0.5, 0.21875, ((1, 4),)),
        "w_down": normal_values(key_list[8], (FF, D), FF ** -0.5, 0.1875, ((0, 4),)),
        "doc_lengths": jax.vmap(lambda own: ragged(own, SLOTS, TOK_DEV, LONGEST, 2))(jax.random.split(key_list[9], BLOCKS)).reshape((BLOCKS, SLOTS)).astype(jnp.int32),
    }


@jax.custom_vjp
def low(v):
    return lax.optimization_barrier(v.astype(jnp.bfloat16)).astype(jnp.float32)

@jax.custom_vjp
def low_back(v):
    return v

def low_keep(v):
    return (low(v), None)

def low_pass(kept, grad):
    return (grad,)

def back_keep(v):
    return (v, None)

def back_low(kept, grad):
    return (low(grad),)
low.defvjp(low_keep, low_pass)
low_back.defvjp(back_keep, back_low)
eps_norm = 1e-05
theta_rope = 160000.0
highest = lax.Precision.HIGHEST

def matmul(left, right):
    return jnp.matmul(left, right, precision=highest)

def layout(doc_lengths):
    doc_ends = jnp.cumsum(doc_lengths, axis=1).astype(jnp.int32)
    starts = doc_ends - doc_lengths
    places = jnp.arange(TOK_DEV, dtype=jnp.int32)
    doc_ids = lax.optimization_barrier(jnp.sum((places[None, :, None] >= doc_ends[:, None, :]).astype(jnp.int32), axis=2))
    picked = doc_ids[:, :, None] == jnp.arange(SLOTS, dtype=jnp.int32)[None, None, :]
    offsets = lax.optimization_barrier(jnp.sum(jnp.where(picked, starts[:, None, :], 0), axis=2))
    real_rows = (doc_ids < DOCS).astype(jnp.float32)
    return (doc_ids, places[None, :] - offsets, real_rows)

def rope_tables(positions):
    half_dim = HEAD_DIM // 2
    frequency = jnp.exp(jnp.arange(half_dim, dtype=jnp.float32) * (-2.0 * math.log(theta_rope) / HEAD_DIM))
    angles = positions.astype(jnp.float32)[..., None] * frequency
    cos_table = jnp.concatenate([jnp.cos(angles), jnp.cos(angles)], axis=-1)
    sin_table = jnp.concatenate([jnp.sin(angles), jnp.sin(angles)], axis=-1)
    return (cos_table, sin_table)

def rotate_half(vector):
    half_dim = vector.shape[-1] // 2
    return jnp.concatenate([-vector[..., half_dim:], vector[..., :half_dim]], axis=-1)

def apply_rope(vector, cos_table, sin_table):
    return vector * cos_table + rotate_half(vector) * sin_table

def layer_norm(value, gain):
    mean_value = lax.optimization_barrier(jnp.mean(value, axis=-1, keepdims=True))
    centered = value - mean_value
    inverse = lax.rsqrt(lax.optimization_barrier(jnp.mean(centered * centered, axis=-1, keepdims=True)) + eps_norm)
    return centered * inverse * gain

def gelu_exact(value):
    return 0.5 * value * (1.0 + lax.erf(value * (1.0 / math.sqrt(2.0))))

def block_attention(inputs):
    queries, key_rows, values, doc_ids = inputs
    scores = jnp.einsum('qhd,khd->hqk', queries, key_rows, precision=highest) * (1.0 / math.sqrt(HEAD_DIM))
    scores = low_back(scores)
    allowed = doc_ids[:, None] == doc_ids[None, :]
    masked = jnp.where(allowed[None], scores, -1e+30)
    top_score = lax.optimization_barrier(jnp.max(masked, axis=2, keepdims=True))
    weights = jnp.exp(masked - top_score)
    attention = low(weights / lax.optimization_barrier(jnp.sum(weights, axis=2, keepdims=True)))
    return jnp.einsum('hqk,khd->qhd', attention, values, precision=highest)

def forward(hidden_in, w_qkv, w_attn_out, attn_gain, mlp_gain, w_gate, w_up, w_down, doc_ids, cos_table, sin_table, real_rows):
    input_one = low(layer_norm(hidden_in, attn_gain))
    projected = low_back(matmul(input_one, w_qkv))
    split_qkv = projected.reshape(BLOCKS, TOK_DEV, 3, HEADS, HEAD_DIM)
    queries = low(apply_rope(split_qkv[:, :, 0], cos_table, sin_table))
    key_rows = low(apply_rope(split_qkv[:, :, 1], cos_table, sin_table))
    values = low(split_qkv[:, :, 2])
    mixed = lax.map(jax.checkpoint(block_attention), (queries, key_rows, values, doc_ids))
    mixed = mixed.reshape(TOKENS, D) * real_rows.reshape(TOKENS, 1)
    attended = low(low_back(mixed))
    hidden_mid = hidden_in + low_back(matmul(attended, w_attn_out))
    input_two = low(layer_norm(hidden_mid, mlp_gain))
    gate_pre = low_back(matmul(input_two, w_gate))
    up_pre = low_back(matmul(input_two, w_up))
    inner = low(gelu_exact(gate_pre) * up_pre)
    return hidden_mid + low_back(matmul(inner, w_down))

def reference(hidden_in, cotangent, w_qkv, w_attn_out, attn_gain, mlp_gain, w_gate, w_up, w_down, doc_lengths):
    doc_ids, positions, real_rows = layout(doc_lengths)
    cos_table, sin_table = rope_tables(positions)
    cos_table = cos_table[:, :, None, :]
    sin_table = sin_table[:, :, None, :]
    float_args = tuple((array.astype(jnp.float32) for array in (hidden_in, w_qkv, w_attn_out, attn_gain, mlp_gain, w_gate, w_up, w_down)))

    def apply_layer(hidden_arg, qkv_arg, out_arg, gain_one, gain_two, gate_arg, up_arg, down_arg):
        return forward(hidden_arg, qkv_arg, out_arg, gain_one, gain_two, gate_arg, up_arg, down_arg, doc_ids, cos_table, sin_table, real_rows)
    layer_value, pullback = jax.vjp(apply_layer, *float_args)
    gradients = pullback(cotangent.astype(jnp.float32) * real_rows.reshape(TOKENS, 1))
    return (layer_value.astype(jnp.bfloat16), gradients[0].astype(jnp.bfloat16), gradients[1], gradients[2], gradients[3], gradients[4], gradients[5], gradients[6], gradients[7])
```

```python
import math

import jax
import jax.numpy as jnp
from jax import lax
from jax.sharding import PartitionSpec as P

HEADS = 12
HEAD_DIM = 64


eps_norm = 1e-05
theta_rope = 160000.0
contract_rows = (((0,), (0,)), ((), ()))
contract_cols = (((1,), (1,)), ((), ()))
bf16 = jnp.bfloat16
f32 = jnp.float32


def layout(doc_lengths, row_count):
    lengths = doc_lengths[0]
    slot_count = lengths.shape[0]
    doc_ends = jnp.cumsum(lengths)
    starts = doc_ends - lengths
    places = jnp.arange(row_count, dtype=jnp.int32)
    doc_ids = jnp.sum((places[:, None] >= doc_ends[None, :]).astype(jnp.int32), axis=1)
    picked = doc_ids[:, None] == jnp.arange(slot_count, dtype=jnp.int32)[None, :]
    offsets = jnp.sum(jnp.where(picked, starts[None, :], 0), axis=1)
    return (doc_ids, places - offsets, doc_ids < slot_count - 1)


def rope_tables(positions):
    half_dim = HEAD_DIM // 2
    frequency = jnp.exp(
        jnp.arange(half_dim, dtype=jnp.float32) * (-2.0 * math.log(theta_rope) / HEAD_DIM)
    )
    angles = positions.astype(jnp.float32)[..., None] * frequency
    cos_table = jnp.concatenate([jnp.cos(angles), jnp.cos(angles)], axis=-1)
    sin_table = jnp.concatenate([jnp.sin(angles), jnp.sin(angles)], axis=-1)
    return (cos_table, sin_table)


def rotate_half(vector):
    half_dim = vector.shape[-1] // 2
    return jnp.concatenate([-vector[..., half_dim:], vector[..., :half_dim]], axis=-1)


def rotate_back(vector):
    half_dim = vector.shape[-1] // 2
    return jnp.concatenate([vector[..., half_dim:], -vector[..., :half_dim]], axis=-1)


def standardize(value):
    mean_value = jnp.mean(value, axis=-1, keepdims=True)
    centered = value - mean_value
    inverse = lax.rsqrt(jnp.mean(centered * centered, axis=-1, keepdims=True) + eps_norm)
    return (centered * inverse, inverse)


def norm_back(grad_normed, normed, inverse, gain):
    scaled = grad_normed * gain
    return inverse * (
        scaled
        - jnp.mean(scaled, axis=-1, keepdims=True)
        - normed * jnp.mean(scaled * normed, axis=-1, keepdims=True)
    )


def gelu_exact(value):
    return 0.5 * value * (1.0 + lax.erf(value * (1.0 / math.sqrt(2.0))))


def geglu_back(grad_inner, gate_pre, up_pre):
    cumulative = 0.5 * (1.0 + lax.erf(gate_pre * (1.0 / math.sqrt(2.0))))
    density = jnp.exp(-0.5 * gate_pre * gate_pre) * (1.0 / math.sqrt(2.0 * math.pi))
    slope = cumulative + gate_pre * density
    grad_gate = (grad_inner * up_pre * slope).astype(jnp.bfloat16)
    grad_up = (grad_inner * (gate_pre * cumulative)).astype(jnp.bfloat16)
    return (grad_gate, grad_up)


class Links:
    def __init__(self, seq_size, mlp_size):
        self.seq_size, self.mlp_size = seq_size, mlp_size
        self.seq, self.mlp = lax.axis_index("seq"), lax.axis_index("mlp")
        self.seq_bits = seq_size.bit_length() - 1
        self.mlp_bits = mlp_size.bit_length() - 1
        self.low = self.seq & 1

    def stages(self, bits):
        upper = list(range(1, bits))
        out = []
        while len(upper) >= 2:
            one, two = upper[0], upper[1]
            out += [(two, one), (one, two)]
            upper = upper[2:]
        return out + [(bit, bit) for bit in upper]

    def swap_seq(self, value, even_bit, odd_bit):
        pairs = [(i, i ^ (1 << (odd_bit if i & 1 else even_bit))) for i in range(self.seq_size)]
        return lax.ppermute(value, "seq", pairs)

    def swap_mlp(self, value, bit):
        pairs = [(i, i ^ (1 << bit)) for i in range(self.mlp_size)]
        return lax.ppermute(value, "mlp", pairs)

    def seq_bit(self, even_bit, odd_bit):
        return (self.seq >> jnp.where(self.low == 1, odd_bit, even_bit)) & 1

    @staticmethod
    def pair(mine, other, bit):
        first = jnp.where(bit == 0, mine, other)
        second = jnp.where(bit == 0, other, mine)
        return jnp.stack([first, second])

    def absolute(self, bits, which):
        return [stage[which] for stage in reversed(self.stages(bits))]

    def gather(self, unit, bits):
        shape = unit.shape
        value = unit
        for bit in range(self.mlp_bits):
            value = self.pair(value, self.swap_mlp(value, bit), (self.mlp >> bit) & 1)
        value = value.reshape((self.mlp_size,) + shape)
        for even_bit, odd_bit in self.stages(bits):
            other = self.swap_seq(value, even_bit, odd_bit)
            value = self.pair(value, other, self.seq_bit(even_bit, odd_bit))
        other = self.swap_seq(value, 0, 0)
        halves = self.pair(value, other, self.low)
        sorted_halves = []
        for which in (0, 1):
            order = self.absolute(bits, which)
            places = [order.index(bit) for bit in range(bits - 1, 0, -1)]
            rest = list(range(len(order), len(order) + 1 + len(shape)))
            sorted_halves.append(jnp.transpose(halves[which], places + rest))
        return jnp.stack(sorted_halves, axis=bits - 1).reshape((1 << bits, self.mlp_size) + shape)

    def scatter_sum(self, value, bits):
        shape = value.shape[2:]
        value = value.reshape((2,) * bits + (self.mlp_size,) + shape)
        halves = []
        for which in (0, 1):
            half = lax.index_in_dim(value, which, bits - 1, keepdims=False)
            order = self.absolute(bits, which)
            rest = list(range(bits - 1, bits - 1 + 1 + len(shape)))
            halves.append(jnp.transpose(half, [bits - 1 - bit for bit in order] + rest))
        mine = jnp.where(self.low == 0, halves[0], halves[1])
        away = jnp.where(self.low == 0, halves[1], halves[0]).astype(bf16)
        value = mine + self.swap_seq(away, 0, 0).astype(f32)
        for even_bit, odd_bit in reversed(self.stages(bits)):
            bit = self.seq_bit(even_bit, odd_bit)
            mine = jnp.where(bit == 0, value[0], value[1])
            away = jnp.where(bit == 0, value[1], value[0]).astype(bf16)
            value = mine + self.swap_seq(away, even_bit, odd_bit).astype(f32)
        value = value.reshape((2,) * self.mlp_bits + shape)
        for bit in reversed(range(self.mlp_bits)):
            own = (self.mlp >> bit) & 1
            mine = jnp.where(own == 0, value[0], value[1])
            away = jnp.where(own == 0, value[1], value[0]).astype(bf16)
            value = mine + self.swap_mlp(away, bit).astype(f32)
        return value

    def total(self, value):
        for bit in range(self.seq_bits):
            value = value + self.swap_seq(value, bit, bit)
        for bit in range(self.mlp_bits):
            value = value + self.swap_mlp(value, bit)
        return value


def after(value, *others):
    return lax.optimization_barrier((value,) + others)[0]


def pad_rows(value, rows):
    return jnp.pad(value, ((0, rows - value.shape[0]), (0, 0)))


def up_to(value, step):
    return -(-value // step) * step


def make_shards(seq_size, mlp_size):
    def shards(
        hidden_in,
        cotangent,
        w_qkv,
        w_attn_out,
        attn_gain,
        mlp_gain,
        w_gate,
        w_up,
        w_down,
        doc_lengths,
    ):
        links = Links(seq_size, mlp_size)
        devices = seq_size * mlp_size
        row_count = hidden_in.shape[0]
        model_dim = hidden_in.shape[1]
        units = w_down.shape[0]
        hidden_units = units * mlp_size
        scale_score = 1.0 / math.sqrt(HEAD_DIM)

        qkv_part = w_qkv.shape[1]
        out_part = w_attn_out.shape[1]
        gain_part = attn_gain.shape[0]
        qkv_rows = up_to(qkv_part + 1, 16)
        gains = jnp.concatenate([attn_gain, mlp_gain])
        gains = jnp.pad(gains, (0, model_dim - gains.shape[0]))
        unit_qkv = pad_rows(jnp.concatenate([w_qkv.T, gains[None]]), qkv_rows)
        all_qkv = links.gather(unit_qkv, links.seq_bits).reshape(devices, qkv_rows, model_dim)
        full_qkv = all_qkv[:, :qkv_part].reshape(3 * model_dim, model_dim)
        gain_rows = all_qkv[:, qkv_part]
        gain_attn = gain_rows[:, :gain_part].reshape(model_dim).astype(f32)
        gain_mlp = gain_rows[:, gain_part : 2 * gain_part].reshape(model_dim).astype(f32)

        share_bits = min(3, links.seq_bits)
        shares = 1 << share_bits
        share_rows = up_to(up_to(3 * units, shares) // shares, 16)
        local_ff = pad_rows(jnp.concatenate([w_gate.T, w_up.T, w_down]), share_rows * shares)
        unit_ff = lax.dynamic_slice_in_dim(
            local_ff, (links.seq % shares) * share_rows, share_rows, axis=0
        )
        unit_out = pad_rows(w_attn_out.T, up_to(out_part, 16))
        unit_out = after(unit_out, full_qkv)
        all_out = links.gather(unit_out, links.seq_bits)
        full_out = all_out.reshape((devices,) + unit_out.shape)[:, :out_part]
        full_out = full_out.reshape(model_dim, model_dim)
        unit_ff = after(unit_ff, full_out)
        all_ff = jnp.swapaxes(links.gather(unit_ff, share_bits), 0, 1)
        all_ff = all_ff.reshape(mlp_size, share_rows * shares, model_dim)
        full_gate = all_ff[:, :units].reshape(hidden_units, model_dim)
        full_up = all_ff[:, units : 2 * units].reshape(hidden_units, model_dim)
        full_down = all_ff[:, 2 * units : 3 * units].reshape(hidden_units, model_dim)

        doc_ids, positions, real_mask = layout(doc_lengths, row_count)
        real_rows = real_mask.astype(jnp.float32)
        cos_table, sin_table = rope_tables(positions)
        cos_heads = cos_table[:, None, :]
        sin_heads = sin_table[:, None, :]
        allowed = doc_ids[:, None] == doc_ids[None, :]
        hidden_first = hidden_in.astype(jnp.float32)
        normed_one, inverse_one = standardize(hidden_first)
        input_one = (normed_one * gain_attn).astype(jnp.bfloat16)
        projected = lax.dot_general(
            input_one, full_qkv, contract_cols, preferred_element_type=jnp.float32
        )
        split_qkv = projected.reshape(row_count, 3, HEADS, HEAD_DIM)
        query_rows = (
            split_qkv[:, 0] * cos_heads + rotate_half(split_qkv[:, 0]) * sin_heads
        ).astype(jnp.bfloat16)
        key_rows = (split_qkv[:, 1] * cos_heads + rotate_half(split_qkv[:, 1]) * sin_heads).astype(
            jnp.bfloat16
        )
        value_rows = split_qkv[:, 2].astype(jnp.bfloat16)
        query_heads = jnp.swapaxes(query_rows, 0, 1)
        key_heads = jnp.swapaxes(key_rows, 0, 1)
        value_heads = jnp.swapaxes(value_rows, 0, 1)

        def head_forward(inputs):
            query_one, key_one, value_one = inputs
            scores = (
                jnp.einsum("qd,kd->qk", query_one, key_one, preferred_element_type=jnp.float32)
                * scale_score
            )
            masked = jnp.where(allowed, scores, -1e30)
            top_score = jnp.max(masked, axis=1, keepdims=True)
            weights = jnp.exp(masked - top_score)
            total = jnp.sum(weights, axis=1, keepdims=True)
            attention = (weights / total).astype(jnp.bfloat16)
            mixed_one = jnp.dot(attention, value_one, preferred_element_type=jnp.float32)
            return (mixed_one, top_score[:, 0] + jnp.log(total[:, 0]))

        mixed_heads, log_totals = lax.map(head_forward, (query_heads, key_heads, value_heads))
        mixed = jnp.swapaxes(mixed_heads, 0, 1).reshape(row_count, model_dim)
        attended = (mixed * real_rows[:, None]).astype(jnp.bfloat16)
        hidden_mid = hidden_first + lax.dot_general(
            attended, full_out, contract_cols, preferred_element_type=jnp.float32
        )
        normed_two, inverse_two = standardize(hidden_mid)
        input_two = (normed_two * gain_mlp).astype(jnp.bfloat16)
        grad_top = cotangent.astype(jnp.float32) * real_rows[:, None]
        grad_low = grad_top.astype(jnp.bfloat16)

        gate_pre = lax.dot_general(input_two, full_gate, contract_cols, preferred_element_type=f32)
        up_pre = lax.dot_general(input_two, full_up, contract_cols, preferred_element_type=f32)
        inner = (gelu_exact(gate_pre) * up_pre).astype(jnp.bfloat16)
        ffn_out = jnp.dot(inner, full_down, preferred_element_type=jnp.float32)
        layer_out = (hidden_mid + ffn_out).astype(jnp.bfloat16)
        down_part = lax.dot_general(inner, grad_low, contract_rows, preferred_element_type=f32)
        grad_inner = lax.dot_general(grad_low, full_down, contract_cols, preferred_element_type=f32)
        grad_gate_rows, grad_up_rows = geglu_back(grad_inner, gate_pre, up_pre)
        gate_part = lax.dot_general(
            grad_gate_rows, input_two, contract_rows, preferred_element_type=f32
        )
        up_part = lax.dot_general(grad_up_rows, input_two, contract_rows, preferred_element_type=f32)
        grad_normed_two = jnp.dot(grad_gate_rows, full_gate, preferred_element_type=f32) + jnp.dot(
            grad_up_rows, full_up, preferred_element_type=f32
        )
        grads_ff = jnp.concatenate(
            [
                part.astype(bf16).reshape(mlp_size, units, model_dim)
                for part in (gate_part, up_part, down_part)
            ],
            axis=1,
        )
        seq_rows = up_to(3 * units, seq_size * 16) // seq_size
        grads_ff = jnp.pad(grads_ff, ((0, 0), (0, seq_rows * seq_size - 3 * units), (0, 0)))
        grads_ff = jnp.swapaxes(
            grads_ff.reshape(mlp_size, seq_size, seq_rows, model_dim), 0, 1
        ).reshape(seq_size * mlp_size * seq_rows, model_dim)
        grads_ff = lax.psum_scatter(grads_ff, "seq", scatter_dimension=0, tiled=True)
        grads_ff = lax.psum_scatter(grads_ff, "mlp", scatter_dimension=0, tiled=True)
        grads_ff = lax.all_gather(grads_ff, "seq", axis=0, tiled=True).astype(f32)
        grad_gate_sum = grads_ff[:units].T
        grad_up_sum = grads_ff[units : 2 * units].T
        grad_down_sum = grads_ff[2 * units : 3 * units]

        grad_gain_mlp = jnp.sum(grad_normed_two * normed_two, axis=0)
        grad_mid = grad_top + norm_back(grad_normed_two, normed_two, inverse_two, gain_mlp)
        grad_mid_low = grad_mid.astype(jnp.bfloat16)
        out_grad = lax.dot_general(
            grad_mid_low, attended, contract_rows, preferred_element_type=jnp.float32
        )
        grad_attn_out = links.scatter_sum(
            out_grad.reshape(seq_size, mlp_size, out_part, model_dim), links.seq_bits
        ).T
        grad_attended = jnp.dot(grad_mid_low, full_out, preferred_element_type=jnp.float32)
        grad_mixed = jnp.where(
            real_mask[:, None], grad_attended.astype(jnp.bfloat16), jnp.zeros((), jnp.bfloat16)
        )
        grad_heads = jnp.swapaxes(grad_mixed.reshape(row_count, HEADS, HEAD_DIM), 0, 1)

        def head_backward(inputs):
            query_one, key_one, value_one, grad_one, log_one = inputs
            scores = (
                jnp.einsum("qd,kd->qk", query_one, key_one, preferred_element_type=jnp.float32)
                * scale_score
            )
            attention = jnp.where(allowed, jnp.exp(scores - log_one[:, None]), 0.0)
            attention_low = attention.astype(jnp.bfloat16)
            grad_value = lax.dot_general(
                attention_low, grad_one, contract_rows, preferred_element_type=jnp.float32
            )
            grad_attention = jnp.einsum(
                "qd,kd->qk", grad_one, value_one, preferred_element_type=jnp.float32
            )
            row_terms = jnp.sum(attention * grad_attention, axis=1, keepdims=True)
            grad_scores = (attention * (grad_attention - row_terms)).astype(jnp.bfloat16)
            grad_query = (
                jnp.dot(grad_scores, key_one, preferred_element_type=jnp.float32) * scale_score
            )
            grad_key = (
                lax.dot_general(
                    grad_scores, query_one, contract_rows, preferred_element_type=jnp.float32
                )
                * scale_score
            )
            return (grad_query, grad_key, grad_value)

        grad_query_heads, grad_key_heads, grad_value_heads = lax.map(
            head_backward, (query_heads, key_heads, value_heads, grad_heads, log_totals)
        )
        grad_query_rows = jnp.swapaxes(grad_query_heads, 0, 1)
        grad_key_rows = jnp.swapaxes(grad_key_heads, 0, 1)
        grad_value_rows = jnp.swapaxes(grad_value_heads, 0, 1)
        grad_query_pre = grad_query_rows * cos_heads + rotate_back(grad_query_rows * sin_heads)
        grad_key_pre = grad_key_rows * cos_heads + rotate_back(grad_key_rows * sin_heads)
        grad_projected = (
            jnp.stack([grad_query_pre, grad_key_pre, grad_value_rows], axis=1)
            .reshape(row_count, 3 * model_dim)
            .astype(jnp.bfloat16)
        )
        qkv_grad = lax.dot_general(
            grad_projected, input_one, contract_rows, preferred_element_type=jnp.float32
        )
        grad_qkv = links.scatter_sum(
            qkv_grad.reshape(seq_size, mlp_size, qkv_part, model_dim), links.seq_bits
        ).T
        grad_normed_one = jnp.dot(grad_projected, full_qkv, preferred_element_type=jnp.float32)
        grad_gain_attn = jnp.sum(grad_normed_one * normed_one, axis=0)
        grad_hidden = (
            grad_mid + norm_back(grad_normed_one, normed_one, inverse_one, gain_attn)
        ).astype(jnp.bfloat16)
        gain_grads = links.total(jnp.stack([grad_gain_attn, grad_gain_mlp]))
        own_gain = (links.seq * mlp_size + links.mlp) * gain_part
        gain_grads = lax.dynamic_slice_in_dim(gain_grads, own_gain, gain_part, axis=1)
        return (
            layer_out,
            grad_hidden,
            grad_qkv,
            grad_attn_out,
            gain_grads[0],
            gain_grads[1],
            grad_gate_sum,
            grad_up_sum,
            grad_down_sum,
        )

    return shards


def solution(mesh):
    both = ("seq", "mlp")
    in_specs = (
        P(both, None),
        P(both, None),
        P(None, both),
        P(None, both),
        P(both),
        P(both),
        P(None, "mlp"),
        P(None, "mlp"),
        P("mlp", None),
        P(both, None),
    )
    out_specs = (
        P(both, None),
        P(both, None),
        P(None, both),
        P(None, both),
        P(both),
        P(both),
        P(None, "mlp"),
        P(None, "mlp"),
        P("mlp", None),
    )
    body = make_shards(mesh.shape["seq"], mesh.shape["mlp"])
    return jax.shard_map(body, mesh=mesh, in_specs=in_specs, out_specs=out_specs, check_vma=False)
```

```python
import functools
import math

import jax
import jax.numpy as jnp
from jax import lax
from jax.experimental import pallas as pl
from jax.experimental.pallas import tpu as pltpu
from jax.sharding import PartitionSpec as P

HEADS = 12
HEAD_DIM = 64


eps_norm = 1e-05
theta_rope = 160000.0
contract_rows = (((0,), (0,)), ((), ()))
contract_cols = (((1,), (1,)), ((), ()))
bf16 = jnp.bfloat16
f32 = jnp.float32


def layout(doc_lengths, row_count):
    lengths = doc_lengths[0]
    slot_count = lengths.shape[0]
    doc_ends = jnp.cumsum(lengths)
    starts = doc_ends - lengths
    places = jnp.arange(row_count, dtype=jnp.int32)
    doc_ids = jnp.sum((places[:, None] >= doc_ends[None, :]).astype(jnp.int32), axis=1)
    picked = doc_ids[:, None] == jnp.arange(slot_count, dtype=jnp.int32)[None, :]
    offsets = jnp.sum(jnp.where(picked, starts[None, :], 0), axis=1)
    return (doc_ids, places - offsets, doc_ids < slot_count - 1)


def standardize(value):
    mean_value = jnp.mean(value, axis=-1, keepdims=True)
    centered = value - mean_value
    inverse = lax.rsqrt(jnp.mean(centered * centered, axis=-1, keepdims=True) + eps_norm)
    return (centered * inverse, inverse)


def norm_back(grad_normed, normed, inverse, gain):
    scaled = grad_normed * gain
    return inverse * (
        scaled
        - jnp.mean(scaled, axis=-1, keepdims=True)
        - normed * jnp.mean(scaled * normed, axis=-1, keepdims=True)
    )


def gelu_exact(value):
    return 0.5 * value * (1.0 + lax.erf(value * (1.0 / math.sqrt(2.0))))


def geglu_back(grad_inner, gate_pre, up_pre):
    cumulative = 0.5 * (1.0 + lax.erf(gate_pre * (1.0 / math.sqrt(2.0))))
    density = jnp.exp(-0.5 * gate_pre * gate_pre) * (1.0 / math.sqrt(2.0 * math.pi))
    slope = cumulative + gate_pre * density
    grad_gate = (grad_inner * up_pre * slope).astype(jnp.bfloat16)
    grad_up = (grad_inner * (gate_pre * cumulative)).astype(jnp.bfloat16)
    return (grad_gate, grad_up)


PAIR = 128
TILE = 128
NT = (((1,), (1,)), ((), ()))
NN = (((1,), (0,)), ((), ()))
BLOCKED = -1e30

def swap_halves(value, lane):
    return jnp.where(lane % HEAD_DIM < HEAD_DIM // 2, pltpu.roll(value, PAIR - HEAD_DIM // 2, 1), pltpu.roll(value, HEAD_DIM // 2, 1))

def pieces(value, lane, first):
    high = value.astype(bf16).astype(f32)
    rest = value - high
    middle = rest.astype(bf16).astype(f32)
    last = rest - middle
    place = lane % HEAD_DIM
    return jnp.where(place == first, high, jnp.where(place == first + 1, middle, jnp.where(place == first + 2, last, 0.0)))

def stack_heads(value, lane):
    zero = jnp.zeros_like(value)
    return jnp.concatenate([jnp.where(lane % PAIR < HEAD_DIM, value, zero), jnp.where(lane % PAIR < HEAD_DIM, zero, value)], axis=0)

def forward_kernel(x_ref, wq_ref, wk_ref, wv_ref, cos_ref, sin_ref, docs_q_ref, docs_k_ref, real_ref, *refs):
    q_ref, k_ref, v_ref, o_ref, aug_ref, w_s, k_s, vt_s, s_a, s_b, top_s = refs[-11:]
    rows = x_ref.shape[0]
    lane = lax.broadcasted_iota(jnp.int32, (rows, PAIR), 1)
    w_s[0:PAIR] = wq_ref[...]
    w_s[PAIR:2*PAIR] = wk_ref[...]
    x = x_ref[...]
    both = lax.dot_general(x, w_s[...], NT, preferred_element_type=f32)
    value = lax.dot_general(x, wv_ref[...], NT, preferred_element_type=f32)
    cos = cos_ref[...]; sin = sin_ref[...]
    query = both[:, :PAIR]; key = both[:, PAIR:]
    query = (query * cos + swap_halves(query, lane) * sin).astype(bf16)
    key = (key * cos + swap_halves(key, lane) * sin).astype(bf16)
    q_ref[...] = query * jnp.asarray(0.125, bf16)
    k_ref[...] = key
    v_ref[...] = value.astype(bf16)
    k_s[:, :PAIR] = key
    k_s[:, PAIR:] = docs_k_ref[...]
    vt_s[0:PAIR] = value.T.astype(bf16)
    vt_s[PAIR:] = jnp.ones((vt_s.shape[0]-PAIR, rows), bf16)
    lane2 = lax.broadcasted_iota(jnp.int32, (TILE, 2*PAIR), 1)
    sub = lax.broadcasted_iota(jnp.int32, (PAIR, TILE), 0)
    lane1 = lax.broadcasted_iota(jnp.int32, (TILE, PAIR), 1)

    def start(i, slot):
        at = pl.ds(pl.multiple_of(i * TILE, TILE), TILE)
        q_tile = jnp.concatenate([q_ref[at, :], docs_q_ref[at, :]], axis=1)
        q_cat = stack_heads(q_tile, lane2)
        scores = lax.dot_general(k_s[...], q_cat, NT, preferred_element_type=f32)
        (s_a, s_b)[slot][...] = scores
        top_s[slot] = jnp.broadcast_to(jnp.max(scores, axis=0, keepdims=True), (8, 2 * TILE))

    def finish(i, slot):
        at = pl.ds(pl.multiple_of(i * TILE, TILE), TILE)
        top = top_s[slot][0:1]
        weights = jnp.exp((s_a, s_b)[slot][...] - top).astype(bf16)
        mixed = lax.dot_general(vt_s[...], weights, NN, preferred_element_type=f32)
        total = mixed[PAIR:PAIR+1]
        out = mixed[:PAIR] * (1.0 / total)
        out = jnp.where(sub < HEAD_DIM, out[:, :TILE], out[:, TILE:])
        o_ref[at, :] = (out.T * real_ref[at, :]).astype(bf16)
        log_total = top + jnp.log(total)
        log_total = jnp.where(sub < HEAD_DIM, log_total[:, :TILE], log_total[:, TILE:])
        aug_ref[at, :] = docs_q_ref[at, :] + pieces(log_total.T, lane1, 5).astype(bf16)

    count = rows // TILE
    start(0, 0)

    def step(i, carry):
        start(2 * i + 1, 1)
        finish(2 * i, 0)
        start(2 * i + 2, 0)
        finish(2 * i + 1, 1)
        return carry
    lax.fori_loop(0, (count - 1) // 2, step, 0)
    if count % 2 == 0:
        start(count - 1, 1)
        finish(count - 2, 0)
        finish(count - 1, 1)
    else:
        finish(count - 1, 0)

def backward_kernel(q_ref, k_ref, v_ref, o_ref, aug_ref, g_ref, cos_ref, sin_ref, docs_k_ref, ones_ref, *refs):
    out_ref, k_s, v_s, kt_s, dk_s, dv_s = refs[-6:]
    rows = q_ref.shape[0]
    lane = lax.broadcasted_iota(jnp.int32, (rows, PAIR), 1)
    lane1 = lax.broadcasted_iota(jnp.int32, (TILE, PAIR), 1)
    lane2 = lax.broadcasted_iota(jnp.int32, (TILE, 2*PAIR), 1)
    sub = lax.broadcasted_iota(jnp.int32, (PAIR, TILE), 0)
    k_s[:, :PAIR] = k_ref[...]
    k_s[:, PAIR:] = docs_k_ref[...]
    v_s[:, :PAIR] = v_ref[...]
    v_s[:, PAIR:] = ones_ref[...]
    kt_s[...] = k_ref[...].astype(f32).T.astype(bf16)
    dk_s[...] = jnp.zeros_like(dk_s)
    dv_s[...] = jnp.zeros_like(dv_s)

    def unrope(value, cos, sin, lane):
        turned = value * sin
        return value * cos + swap_halves(turned, lane)

    def step(i, carry):
        at = pl.ds(pl.multiple_of(i * TILE, TILE), TILE)
        q_cat = stack_heads(jnp.concatenate([q_ref[at, :], aug_ref[at, :]], axis=1), lane2)
        grad = g_ref[at, :]
        product = grad.astype(f32) * o_ref[at, :].astype(f32)
        first = jnp.sum(jnp.where(lane1 < HEAD_DIM, product, 0.0), axis=1, keepdims=True)
        second = jnp.sum(jnp.where(lane1 < HEAD_DIM, 0.0, product), axis=1, keepdims=True)
        row_terms = jnp.where(lane1 < HEAD_DIM, first, second)
        g_aug = pieces(-row_terms, lane1, 0).astype(bf16)
        g_cat = stack_heads(jnp.concatenate([grad, g_aug], axis=1), lane2)
        probs = jnp.exp(lax.dot_general(k_s[...], q_cat, NT, preferred_element_type=f32))
        grad_probs = lax.dot_general(v_s[...], g_cat, NT, preferred_element_type=f32)
        grad_scores = (probs * grad_probs).astype(bf16)
        dv_s[...] += lax.dot_general(probs.astype(bf16), g_cat[:, :PAIR], NN, preferred_element_type=f32)
        dk_s[...] += lax.dot_general(grad_scores, q_cat[:, :PAIR], NN, preferred_element_type=f32)
        dqt = lax.dot_general(kt_s[...], grad_scores, NN, preferred_element_type=f32)
        dq = jnp.where(sub < HEAD_DIM, dqt[:, :TILE], dqt[:, TILE:]).T * 0.125
        out_ref[0, at, :] = unrope(dq, cos_ref[at, :], sin_ref[at, :], lane1).astype(bf16)
        return carry
    lax.fori_loop(0, rows // TILE, step, 0)
    out_ref[1] = unrope(dk_s[...], cos_ref[...], sin_ref[...], lane).astype(bf16)
    out_ref[2] = dv_s[...].astype(bf16)

def cost(flops, size, trans):
    return pl.CostEstimate(flops=flops, bytes_accessed=size, transcendentals=trans)

def attention_forward(x, w, cos, sin, docs_q, docs_k, real, calls):
    rows, dim = x.shape
    pairs = dim // PAIR
    per = pairs // calls
    full = pl.BlockSpec((rows, dim), lambda p: (0, 0))
    one = pl.BlockSpec((rows, PAIR), lambda p: (0, 0))
    outs = None
    shapes = tuple(jax.ShapeDtypeStruct((rows, dim), bf16) for _ in range(5))
    for c in range(calls):
        base = c * per
        wspec = [pl.BlockSpec((PAIR, dim), functools.partial(lambda s, p: (s + p, 0), base + s * pairs)) for s in range(3)]
        ospec = pl.BlockSpec((rows, PAIR), functools.partial(lambda b, p: (0, b + p), base))
        extra = [] if outs is None else list(outs)
        outs = pl.pallas_call(
            forward_kernel, out_shape=shapes, grid=(per,),
            in_specs=[full] + wspec + [one] * 5 + [pl.BlockSpec(memory_space=pl.ANY)] * len(extra),
            out_specs=[ospec] * 5,
            scratch_shapes=[pltpu.VMEM((2 * PAIR, dim), bf16), pltpu.VMEM((rows, 2 * PAIR), bf16), pltpu.VMEM((PAIR + 16, rows), bf16), pltpu.VMEM((rows, 2 * TILE), f32), pltpu.VMEM((rows, 2 * TILE), f32), pltpu.VMEM((2, 8, 2 * TILE), f32)],
            input_output_aliases={9 + i: i for i in range(len(extra))},
            cost_estimate=cost(per * (2 * rows * dim * 3 * PAIR + 8 * rows * rows * PAIR), rows * dim * 4, per * 2 * rows * rows),
            name="attend",
        )(x, w, w, w, cos, sin, docs_q, docs_k, real, *extra)
    return outs

def attention_backward(q, k, v, o, aug, g, cos, sin, docs_k, ones, calls):
    rows, dim = q.shape
    pairs = dim // PAIR
    per = pairs // calls
    one = pl.BlockSpec((rows, PAIR), lambda p: (0, 0))
    out = None
    for c in range(calls):
        base = c * per
        spec = pl.BlockSpec((rows, PAIR), functools.partial(lambda b, p: (0, b + p), base))
        extra = [] if out is None else [out]
        out = pl.pallas_call(
            backward_kernel, out_shape=jax.ShapeDtypeStruct((3, rows, dim), bf16), grid=(per,),
            in_specs=[spec] * 6 + [one] * 4 + [pl.BlockSpec(memory_space=pl.ANY)] * len(extra),
            out_specs=pl.BlockSpec((3, rows, PAIR), functools.partial(lambda b, p: (0, 0, b + p), base)),
            scratch_shapes=[pltpu.VMEM((rows, 2 * PAIR), bf16), pltpu.VMEM((rows, 2 * PAIR), bf16), pltpu.VMEM((PAIR, rows), bf16),
                            pltpu.VMEM((rows, PAIR), f32), pltpu.VMEM((rows, PAIR), f32)],
            input_output_aliases={10: 0} if extra else {},
            cost_estimate=cost(per * 20 * rows * rows * PAIR, rows * dim * 6, per * 2 * rows * rows),
            name="attend_back",
        )(q, k, v, o, aug, g, cos, sin, docs_k, ones, *extra)
    return out

def helper_tables(doc_ids, positions, rows):
    lane = jnp.arange(PAIR)
    half = HEAD_DIM // 2
    freq = jnp.exp((lane % half).astype(f32) * (-2.0 * math.log(theta_rope) / HEAD_DIM))
    ang = positions.astype(f32)[:, None] * freq[None]
    cos = jnp.cos(ang)
    sin = jnp.sin(ang) * jnp.where(lane % HEAD_DIM < half, -1.0, 1.0)[None]
    place = lane % HEAD_DIM
    same = doc_ids[:, None] == place[None]
    docs_q = same.astype(bf16)
    docs_k = jnp.where(place < 5, jnp.where(same, 0.0, BLOCKED), jnp.where(place < 8, -1.0, 0.0)).astype(bf16)
    ones = jnp.broadcast_to(jnp.where(place < 3, 1.0, 0.0), (rows, PAIR)).astype(bf16)
    return cos, sin, docs_q, docs_k, ones


def assemble_kernel(parts, low_ref, mine_ref, other_ref, *out_refs):
    own = low_ref[0] == lax.rem(pl.program_id(0), 2)
    block = jnp.where(own, mine_ref[0], other_ref[0]).astype(f32)
    for (start, rows, flat), out_ref in zip(parts, out_refs):
        if flat:
            pieces_of = [block[i, start : start + rows] for i in range(block.shape[0])]
            out_ref[...] = jnp.concatenate(pieces_of, axis=0).astype(bf16)
        else:
            out_ref[...] = block[:, start : start + rows].astype(bf16)


def assemble(low, mine, other, parts):
    mlp_size, _, dim = mine.shape[-3:]
    mine = mine.reshape((4,) + mine.shape[-3:])
    other = other.reshape((4,) + other.shape[-3:])

    def source(s, low_ref):
        one, two = lax.rem(s // 2, 2), s // 4
        return (jnp.where(lax.rem(s, 2) == 0, one * 2 + two, two * 2 + one), 0, 0, 0)

    spec = pl.BlockSpec((1,) + mine.shape[1:], source)
    shapes, specs = [], []
    for start, rows, flat in parts:
        if flat:
            shapes.append(jax.ShapeDtypeStruct((8 * mlp_size * rows, dim), bf16))
            specs.append(pl.BlockSpec((mlp_size * rows, dim), lambda s, low_ref: (s, 0)))
        else:
            shapes.append(jax.ShapeDtypeStruct((mlp_size, 8 * rows, dim), bf16))
            specs.append(pl.BlockSpec((mlp_size, rows, dim), lambda s, low_ref: (0, s, 0)))
    return pl.pallas_call(
        functools.partial(assemble_kernel, parts),
        out_shape=shapes,
        grid_spec=pltpu.PrefetchScalarGridSpec(
            num_scalar_prefetch=1, grid=(8,), in_specs=[spec, spec], out_specs=specs
        ),
        cost_estimate=pl.CostEstimate(
            flops=mine.size, bytes_accessed=8 * mine.size, transcendentals=0
        ),
        name="assemble",
    )(low.reshape(1), mine, other)


class Links:
    def __init__(self, seq_size, mlp_size):
        self.seq_size, self.mlp_size = seq_size, mlp_size
        self.seq, self.mlp = lax.axis_index("seq"), lax.axis_index("mlp")
        self.seq_bits = seq_size.bit_length() - 1
        self.mlp_bits = mlp_size.bit_length() - 1
        self.low = self.seq & 1

    def stages(self, bits):
        upper = list(range(1, bits))
        out = []
        while len(upper) >= 2:
            one, two = upper[0], upper[1]
            out += [(two, one), (one, two)]
            upper = upper[2:]
        return out + [(bit, bit) for bit in upper]

    def swap_seq(self, value, even_bit, odd_bit):
        pairs = [(i, i ^ (1 << (odd_bit if i & 1 else even_bit))) for i in range(self.seq_size)]
        return lax.ppermute(value, "seq", pairs)

    def swap_mlp(self, value, bit):
        pairs = [(i, i ^ (1 << bit)) for i in range(self.mlp_size)]
        return lax.ppermute(value, "mlp", pairs)

    def seq_bit(self, even_bit, odd_bit):
        return (self.seq >> jnp.where(self.low == 1, odd_bit, even_bit)) & 1

    @staticmethod
    def pair(mine, other, bit):
        first = jnp.where(bit == 0, mine, other)
        second = jnp.where(bit == 0, other, mine)
        return jnp.stack([first, second])

    def absolute(self, bits, which):
        return [stage[which] for stage in reversed(self.stages(bits))]

    def gather_mlp(self, unit):
        value = unit
        for bit in range(self.mlp_bits):
            value = self.pair(value, self.swap_mlp(value, bit), (self.mlp >> bit) & 1)
        return value.reshape((self.mlp_size,) + unit.shape)

    def gather_seq(self, value, bits):
        for even_bit, odd_bit in self.stages(bits):
            other = self.swap_seq(value, even_bit, odd_bit)
            value = self.pair(value, other, self.seq_bit(even_bit, odd_bit))
        return value, self.swap_seq(value, 0, 0)

    def in_order(self, value, other, bits, parts):
        if bits == 3 and all(rows % 8 == 0 and rows * self.mlp_size % 16 == 0 for _, rows, _ in parts):
            return assemble(self.low, value, other, parts)
        shape = value.shape[bits - 1 :]
        halves = self.pair(value, other, self.low)
        sorted_halves = []
        for which in (0, 1):
            order = self.absolute(bits, which)
            places = [order.index(bit) for bit in range(bits - 1, 0, -1)]
            rest = list(range(len(order), len(order) + len(shape)))
            sorted_halves.append(jnp.transpose(halves[which], places + rest))
        joined = jnp.stack(sorted_halves, axis=bits - 1).reshape((1 << bits,) + shape)
        out = []
        for start, rows, flat in parts:
            part = joined[:, :, start : start + rows]
            if not flat:
                part = jnp.swapaxes(part, 0, 1)
                out.append(part.reshape(self.mlp_size, (1 << bits) * rows, shape[-1]))
            else:
                out.append(part.reshape((1 << bits) * self.mlp_size * rows, shape[-1]))
        return out

    def scatter_sum(self, value, bits):
        shape = value.shape[2:]
        value = value.reshape((2,) * bits + (self.mlp_size,) + shape)
        halves = []
        for which in (0, 1):
            half = lax.index_in_dim(value, which, bits - 1, keepdims=False)
            order = self.absolute(bits, which)
            rest = list(range(bits - 1, bits - 1 + 1 + len(shape)))
            halves.append(jnp.transpose(half, [bits - 1 - bit for bit in order] + rest))
        mine = jnp.where(self.low == 0, halves[0], halves[1])
        away = jnp.where(self.low == 0, halves[1], halves[0]).astype(bf16)
        value = mine + self.swap_seq(away, 0, 0).astype(f32)
        for even_bit, odd_bit in reversed(self.stages(bits)):
            bit = self.seq_bit(even_bit, odd_bit)
            mine = jnp.where(bit == 0, value[0], value[1])
            away = jnp.where(bit == 0, value[1], value[0]).astype(bf16)
            value = mine + self.swap_seq(away, even_bit, odd_bit).astype(f32)
        value = value.reshape((2,) * self.mlp_bits + shape)
        for bit in reversed(range(self.mlp_bits)):
            own = (self.mlp >> bit) & 1
            mine = jnp.where(own == 0, value[0], value[1])
            away = jnp.where(own == 0, value[1], value[0]).astype(bf16)
            value = mine + self.swap_mlp(away, bit).astype(f32)
        return value

    def total(self, value):
        for bit in range(self.seq_bits):
            value = value + self.swap_seq(value, bit, bit)
        for bit in range(self.mlp_bits):
            value = value + self.swap_mlp(value, bit)
        return value


def after(value, *others):
    return lax.optimization_barrier((value,) + others)[0]


def pad_rows(value, rows):
    return jnp.pad(value, ((0, rows - value.shape[0]), (0, 0)))


def up_to(value, step):
    return -(-value // step) * step


def make_shards(seq_size, mlp_size):
    def shards(
        hidden_in,
        cotangent,
        w_qkv,
        w_attn_out,
        attn_gain,
        mlp_gain,
        w_gate,
        w_up,
        w_down,
        doc_lengths,
    ):
        links = Links(seq_size, mlp_size)
        devices = seq_size * mlp_size
        row_count = hidden_in.shape[0]
        model_dim = hidden_in.shape[1]
        units = w_down.shape[0]
        hidden_units = units * mlp_size
        qkv_part = w_qkv.shape[1]
        out_part = w_attn_out.shape[1]
        gain_part = attn_gain.shape[0]
        qkv_rows = up_to(qkv_part + 1, 16)
        gains = jnp.concatenate([attn_gain, mlp_gain])
        gains = jnp.pad(gains, (0, model_dim - gains.shape[0]))
        unit_qkv = pad_rows(jnp.concatenate([w_qkv.T, gains[None]]), qkv_rows)
        share_bits = min(3, links.seq_bits)
        shares = 1 << share_bits
        share_rows = up_to(up_to(3 * units, shares) // shares, 16)
        local_ff = pad_rows(jnp.concatenate([w_gate.T, w_up.T, w_down]), share_rows * shares)
        unit_ff = lax.dynamic_slice_in_dim(
            local_ff, (links.seq % shares) * share_rows, share_rows, axis=0
        )
        unit_out = pad_rows(w_attn_out.T, up_to(out_part, 16))
        together = share_bits == links.seq_bits

        near_qkv = links.gather_mlp(unit_qkv)
        if together:
            near_rest = links.gather_mlp(after(jnp.concatenate([unit_ff, unit_out]), near_qkv))
        else:
            near_rest = links.gather_mlp(after(unit_ff, near_qkv))
            near_out = links.gather_mlp(after(unit_out, near_qkv))
        spare = qkv_rows - qkv_part
        full_qkv, gain_rows = links.in_order(
            *links.gather_seq(near_qkv, links.seq_bits),
            links.seq_bits,
            [(0, qkv_part, True), (qkv_part, spare, True)],
        )
        gain_rows = gain_rows.reshape(devices, spare, model_dim)[:, 0]
        gain_attn = gain_rows[:, :gain_part].reshape(model_dim).astype(f32)
        gain_mlp = gain_rows[:, gain_part : 2 * gain_part].reshape(model_dim).astype(f32)
        parts_ff = [(0, share_rows, False)]
        rest_halves = links.gather_seq(after(near_rest, full_qkv), share_bits)
        if together:
            all_ff, full_out = links.in_order(
                *rest_halves, share_bits, parts_ff + [(share_rows, out_part, True)]
            )
        else:
            (all_ff,) = links.in_order(*rest_halves, share_bits, parts_ff)
            (full_out,) = links.in_order(
                *links.gather_seq(after(near_out, full_qkv), links.seq_bits),
                links.seq_bits,
                [(0, out_part, True)],
            )
        full_gate = all_ff[:, :units].reshape(hidden_units, model_dim)
        full_up = all_ff[:, units : 2 * units].reshape(hidden_units, model_dim)
        full_down = all_ff[:, 2 * units : 3 * units].reshape(hidden_units, model_dim)

        doc_ids, positions, real_mask = layout(doc_lengths, row_count)
        real_rows = real_mask.astype(jnp.float32)
        tables = helper_tables(doc_ids, positions, row_count)
        cos_table, sin_table, docs_query, docs_key, ones_value = tables
        hidden_first = hidden_in.astype(jnp.float32)
        normed_one, inverse_one = standardize(hidden_first)
        input_one = (normed_one * gain_attn).astype(jnp.bfloat16)
        real_lanes = jnp.broadcast_to(real_rows[:, None], (row_count, PAIR))
        query_rows, key_rows, value_rows, attended, query_extra = attention_forward(
            input_one, full_qkv, cos_table, sin_table, docs_query, docs_key, real_lanes, 6
        )
        hidden_mid = hidden_first + lax.dot_general(
            attended, full_out, contract_cols, preferred_element_type=jnp.float32
        )
        normed_two, inverse_two = standardize(hidden_mid)
        input_two = (normed_two * gain_mlp).astype(jnp.bfloat16)
        grad_top = cotangent.astype(jnp.float32) * real_rows[:, None]
        grad_low = grad_top.astype(jnp.bfloat16)

        gate_pre = lax.dot_general(input_two, full_gate, contract_cols, preferred_element_type=f32)
        up_pre = lax.dot_general(input_two, full_up, contract_cols, preferred_element_type=f32)
        inner = (gelu_exact(gate_pre) * up_pre).astype(jnp.bfloat16)
        ffn_out = jnp.dot(inner, full_down, preferred_element_type=jnp.float32)
        layer_out = (hidden_mid + ffn_out).astype(jnp.bfloat16)
        down_part = lax.dot_general(inner, grad_low, contract_rows, preferred_element_type=f32)
        grad_inner = lax.dot_general(grad_low, full_down, contract_cols, preferred_element_type=f32)
        grad_gate_rows, grad_up_rows = geglu_back(grad_inner, gate_pre, up_pre)
        gate_part = lax.dot_general(
            grad_gate_rows, input_two, contract_rows, preferred_element_type=f32
        )
        up_part = lax.dot_general(grad_up_rows, input_two, contract_rows, preferred_element_type=f32)
        grad_normed_two = jnp.dot(grad_gate_rows, full_gate, preferred_element_type=f32) + jnp.dot(
            grad_up_rows, full_up, preferred_element_type=f32
        )
        grads_ff = jnp.concatenate(
            [
                part.astype(bf16).reshape(mlp_size, units, model_dim)
                for part in (gate_part, up_part, down_part)
            ],
            axis=1,
        )
        seq_rows = up_to(3 * units, seq_size * 16) // seq_size
        grads_ff = jnp.pad(grads_ff, ((0, 0), (0, seq_rows * seq_size - 3 * units), (0, 0)))
        grads_ff = jnp.swapaxes(
            grads_ff.reshape(mlp_size, seq_size, seq_rows, model_dim), 0, 1
        ).reshape(seq_size * mlp_size * seq_rows, model_dim)
        grads_ff = lax.psum_scatter(grads_ff, "seq", scatter_dimension=0, tiled=True)
        grads_ff = lax.psum_scatter(grads_ff, "mlp", scatter_dimension=0, tiled=True)
        grads_ff = lax.all_gather(grads_ff, "seq", axis=0, tiled=True).astype(f32)
        grad_gate_sum = grads_ff[:units].T
        grad_up_sum = grads_ff[units : 2 * units].T
        grad_down_sum = grads_ff[2 * units : 3 * units]

        grad_gain_mlp = jnp.sum(grad_normed_two * normed_two, axis=0)
        grad_mid = grad_top + norm_back(grad_normed_two, normed_two, inverse_two, gain_mlp)
        grad_mid_low = grad_mid.astype(jnp.bfloat16)
        out_grad = lax.dot_general(
            grad_mid_low, attended, contract_rows, preferred_element_type=jnp.float32
        )
        grad_attn_out = links.scatter_sum(
            out_grad.reshape(seq_size, mlp_size, out_part, model_dim), links.seq_bits
        ).T
        grad_attended = jnp.dot(grad_mid_low, full_out, preferred_element_type=jnp.float32)
        grad_mixed = jnp.where(
            real_mask[:, None], grad_attended.astype(jnp.bfloat16), jnp.zeros((), jnp.bfloat16)
        )
        grad_projected = attention_backward(
            query_rows,
            key_rows,
            value_rows,
            attended,
            query_extra,
            grad_mixed,
            cos_table,
            sin_table,
            docs_key,
            ones_value,
            6,
        )
        qkv_grad = lax.dot_general(
            grad_projected, input_one, (((1,), (0,)), ((), ())), preferred_element_type=jnp.float32
        )
        grad_qkv = links.scatter_sum(
            qkv_grad.reshape(seq_size, mlp_size, qkv_part, model_dim), links.seq_bits
        ).T
        grad_normed_one = lax.dot_general(
            grad_projected,
            full_qkv.reshape(3, model_dim, model_dim),
            (((0, 2), (0, 1)), ((), ())),
            preferred_element_type=jnp.float32,
        )
        grad_gain_attn = jnp.sum(grad_normed_one * normed_one, axis=0)
        grad_hidden = (
            grad_mid + norm_back(grad_normed_one, normed_one, inverse_one, gain_attn)
        ).astype(jnp.bfloat16)
        gain_grads = links.total(jnp.stack([grad_gain_attn, grad_gain_mlp]))
        own_gain = (links.seq * mlp_size + links.mlp) * gain_part
        gain_grads = lax.dynamic_slice_in_dim(gain_grads, own_gain, gain_part, axis=1)
        return (
            layer_out,
            grad_hidden,
            grad_qkv,
            grad_attn_out,
            gain_grads[0],
            gain_grads[1],
            grad_gate_sum,
            grad_up_sum,
            grad_down_sum,
        )

    return shards


def solution(mesh):
    both = ("seq", "mlp")
    in_specs = (
        P(both, None),
        P(both, None),
        P(None, both),
        P(None, both),
        P(both),
        P(both),
        P(None, "mlp"),
        P(None, "mlp"),
        P("mlp", None),
        P(both, None),
    )
    out_specs = (
        P(both, None),
        P(both, None),
        P(None, both),
        P(None, both),
        P(both),
        P(both),
        P(None, "mlp"),
        P(None, "mlp"),
        P("mlp", None),
    )
    body = make_shards(mesh.shape["seq"], mesh.shape["mlp"])
    return jax.shard_map(body, mesh=mesh, in_specs=in_specs, out_specs=out_specs, check_vma=False)
```
